256 devices in a mesh: grp: 8 (over z), blk: 32 (over y, x, core).
Axes of the slice: x: 4, y: 4, z: 8, core: 2. Of those that a mesh axis runs over, the one named last changes fastest.
Arguments:
- inputs: bfloat16 [65536, 128], P(('grp', 'blk')), may hold values from -6 to 6
- targets: bfloat16 [65536], P(('grp', 'blk')), may hold values from -6 to 6
- weight_in: float32 [128, 512], replicated, may hold values from -0.5 to 0.5
- bias_in: float32 [512], replicated, may hold values from -3 to 3
- weight_out: float32 [512, 128], replicated, may hold values from -0.25 to 0.25
- neighbors: int32 [512, 2], replicated, may hold values from 0 to 511, as said below
- owner_map: int32 [512], replicated, may hold values from 0 to 511, as said below
Outputs:
- whitened: float32 [65536], P(('grp', 'blk'))
- trained_in: float32 [128, 512], replicated
- trained_bias: float32 [512], replicated
- trained_out: float32 [512, 128], replicated
The draws below stay inside these ranges and needn't reach their ends.
Inputs may be any that keep to these rules, and one draw needn't show every extreme that they name: A permutation of the block ids: block i is stored at position owner_map[i], which lies on device owner_map[i] // 2 in the grp+blk order. `neighbors`: row p holds the ids of the 2 conditioning blocks of the block at position p: distinct, stored on devices of the same grp index other than the block's own device. Of the 4 conditioning blocks of one device's blocks, at most 1 lie on any one device, and every device takes exactly 1 from some device. In every grp index one block conditions a block on every other device of that grp index.
All inputs are finite; a program needn't handle non-finite values.
Results may differ from the reference program's by a relative error of at most 0.0025.
Values may be sent and summed in bfloat16 or wider, within the bound.
A program may use at most 64 MiB of HBM per device.

```python
import jax
import jax.numpy as jnp
from jax import lax

PTS = 128
IN = 128
HID = 512
FEAT = 128
M = 2
STEPS = 1
BLK_DEV = 2
PEERS = 32
NBLOCKS = 512
POINTS = 65536


def shuffle_others(subkey):
    return jax.random.permutation(subkey, PEERS - 1)


def shuffle_requests(subkey):
    return jax.random.permutation(subkey, BLK_DEV * M)


def block_layout(key):
    device_count = NBLOCKS // BLK_DEV
    regions = device_count // PEERS
    others = PEERS - 1
    subkeys = jax.random.split(jax.random.fold_in(key, 4242), 6)
    owner_map = jax.random.permutation(subkeys[0], NBLOCKS).astype(jnp.int32)
    id_of_position = jnp.zeros((NBLOCKS,), jnp.int32).at[owner_map].set(jnp.arange(NBLOCKS, dtype=jnp.int32))
    hub_peer = jax.random.randint(subkeys[1], (regions,), 0, PEERS)
    hub_local = jax.random.randint(subkeys[2], (regions,), 0, BLK_DEV)
    device = jnp.arange(device_count, dtype=jnp.int32)
    region = device // PEERS
    my_peer = device % PEERS
    hub_here = hub_peer[region]
    hub_offset = (hub_here - my_peer) % PEERS
    offsets = 1 + jax.vmap(shuffle_others)(jax.random.split(subkeys[3], device_count)).astype(jnp.int32)
    scores = jnp.where(offsets == hub_offset[:, None], -1, jnp.arange(others, dtype=jnp.int32)[None, :])
    ordered = jnp.take_along_axis(offsets, jnp.argsort(scores, axis=1), axis=1)
    request_order = jax.vmap(shuffle_requests)(jax.random.split(subkeys[4], device_count)).astype(jnp.int32)
    which_peer = request_order % others
    rank_of = request_order // others
    offset = jnp.take_along_axis(ordered, which_peer, axis=1)
    owner_peer = (my_peer[:, None] + offset) % PEERS
    owner_device = region[:, None] * PEERS + owner_peer
    base_local = jax.random.randint(subkeys[5], (device_count, PEERS), 0, BLK_DEV)
    base_local = jnp.where(jnp.arange(PEERS, dtype=jnp.int32)[None, :] == hub_here[:, None], hub_local[region][:, None], base_local)
    local_index = (jnp.take_along_axis(base_local, owner_peer, axis=1) + rank_of) % BLK_DEV
    position = owner_device * BLK_DEV + local_index
    neighbors = id_of_position[position].reshape(NBLOCKS, M)
    return (owner_map, neighbors.astype(jnp.int32))


def draw_owner_map(key, part):
    return block_layout(key)[0]


def draw_neighbors(key, part):
    return block_layout(key)[1]


def block_levels(rng, dims, cuts, least, top_value):
    level = 1.0
    for axis_at, parts in cuts:
        heights = jax.random.uniform(jax.random.fold_in(jax.random.fold_in(rng, 6), axis_at), (parts,), jnp.float32, least / len(cuts), top_value / len(cuts))
        level = level * jnp.repeat(jnp.exp(heights), dims[axis_at] // parts).reshape((-1,) + (1,) * (len(dims) - 1 - axis_at))
    return level


def normal_values(rng, shape, width, limit, pieces=(), kind=jnp.bfloat16):
    factor_of = block_levels(rng, shape, pieces, -0.22, 0.18) if pieces else 1.0
    entries = jax.random.normal(rng, shape, jnp.float32) * width * factor_of
    return jnp.minimum(jnp.maximum(entries, -limit), limit).astype(kind)


def setup_inputs(seed: int = 0) -> dict:
    key_of = jax.random.split(jax.random.key(seed), 8)
    inputs = normal_values(key_of[0], (POINTS, IN), 1.0, 6.0, ((0, 256),))
    targets = normal_values(key_of[1], (POINTS,), 1.0, 6.0, ((0, 256),))
    weight_in = normal_values(key_of[2], (IN, HID), IN ** -0.5, 0.5, (), jnp.float32)
    bias_in = normal_values(key_of[3], (HID,), 0.5, 3.0, (), jnp.float32)
    weight_out = normal_values(key_of[4], (HID, FEAT), HID ** -0.5, 0.25, (), jnp.float32)
    neighbors = draw_neighbors(jax.random.fold_in(key_of[7], 71), 0)
    owner_map = draw_owner_map(jax.random.fold_in(key_of[7], 71), 0)
    return dict(inputs=inputs, targets=targets, weight_in=weight_in, bias_in=bias_in, weight_out=weight_out, neighbors=neighbors, owner_map=owner_map)


nugget = 0.5
step_length = 3.0
epsilon = 1e-06
highest = lax.Precision.HIGHEST

def silu_slope(preact):
    logistic = jax.nn.sigmoid(preact)
    return logistic * (1.0 + preact * (1.0 - logistic))

def features_of(rows_in, weight_in16, bias_now, weight_out16):
    preact = jnp.dot(rows_in.astype(jnp.float32), weight_in16.astype(jnp.float32), preferred_element_type=jnp.float32) + bias_now
    hidden = jax.nn.silu(preact).astype(jnp.bfloat16)
    features = jnp.dot(hidden.astype(jnp.float32), weight_out16.astype(jnp.float32), preferred_element_type=jnp.float32).astype(jnp.bfloat16)
    return (preact, hidden, features)

def mlp_backward(rows_in, preact, hidden, cotangent, weight_out16):
    grad_out = jnp.dot(hidden.astype(jnp.float32).T, cotangent, precision=highest)
    backed = jnp.dot(cotangent, weight_out16.astype(jnp.float32).T, precision=highest) * silu_slope(preact)
    grad_in = jnp.dot(rows_in.astype(jnp.float32).T, backed, precision=highest)
    return (grad_in, lax.optimization_barrier(jnp.sum(backed, axis=0)), grad_out)

def kernel_part(left_rows, right_rows):
    cross_term = jnp.dot(left_rows, right_rows.T, precision=highest)
    distance = lax.optimization_barrier(jnp.sum(left_rows * left_rows, axis=1))[:, None] + lax.optimization_barrier(jnp.sum(right_rows * right_rows, axis=1))[None, :] - 2.0 * cross_term
    return jnp.exp(distance * (-2.0 / left_rows.shape[1]))

def lower_solve(factor_mat, right_side):
    return lax.linalg.triangular_solve(factor_mat, right_side, left_side=True, lower=True)

def conditional_loss(own_feat, cond_feat, y_block, y_cond):
    eye_c = jnp.eye(cond_feat.shape[0], dtype=cond_feat.dtype)
    eye_b = jnp.eye(own_feat.shape[0], dtype=own_feat.dtype)
    k_cc = kernel_part(cond_feat, cond_feat) + nugget * eye_c
    k_cb = kernel_part(cond_feat, own_feat)
    k_bb = kernel_part(own_feat, own_feat) + nugget * eye_b
    chol_c = jnp.linalg.cholesky(k_cc)
    projected = lower_solve(chol_c, k_cb)
    white_c = lower_solve(chol_c, y_cond[:, None])[:, 0]
    schur_part = k_bb - jnp.dot(projected.T, projected, precision=highest)
    chol_s = jnp.linalg.cholesky(schur_part)
    residual = y_block - jnp.dot(projected.T, white_c, precision=highest)
    white_vec = lower_solve(chol_s, residual[:, None])[:, 0]
    loss_value = 0.5 * jnp.sum(white_vec * white_vec) + jnp.sum(jnp.log(jnp.diagonal(chol_s)))
    return (loss_value, white_vec)

def reference(inputs, targets, weight_in, bias_in, weight_out, neighbors, owner_map):
    block_count = neighbors.shape[0]
    x_blocks = inputs.reshape(block_count, PTS, IN)
    y_blocks = targets.astype(jnp.float32).reshape(block_count, PTS)
    cond_pos = jnp.take(owner_map, neighbors, axis=0).astype(jnp.int32)
    weight = 1.0 / block_count
    params = (weight_in, bias_in, weight_out)
    white_all = jnp.zeros((block_count, PTS), jnp.float32)
    for repeat in range(STEPS):
        weight_in16 = params[0].astype(jnp.bfloat16)
        weight_out16 = params[2].astype(jnp.bfloat16)
        bias_now = params[1]

        def forward(x_block):
            return features_of(x_block, weight_in16, bias_now, weight_out16)[2]
        features = lax.map(forward, x_blocks)

        def per_block(block_index):
            sources = cond_pos[block_index]
            own_feat = features[block_index].astype(jnp.float32)
            cond_feat = jnp.take(features, sources, axis=0).reshape(M * PTS, FEAT).astype(jnp.float32)
            y_block = y_blocks[block_index]
            y_cond = jnp.take(y_blocks, sources, axis=0).reshape(M * PTS)

            def loss_of(first_feat, second_feat):
                return conditional_loss(first_feat, second_feat, y_block, y_cond)
            loss_value, pullback, white_vec = jax.vjp(loss_of, own_feat, cond_feat, has_aux=True)
            cot_b, cot_c = pullback(jnp.ones((), loss_value.dtype) * weight)
            return (cot_b, cot_c.reshape(M, PTS, FEAT).astype(jnp.bfloat16), white_vec)
        cot_own, cot_uses, white_all = lax.map(per_block, jnp.arange(block_count, dtype=jnp.int32))
        total_cot = cot_own + jax.ops.segment_sum(cot_uses.astype(jnp.float32).reshape(block_count * M, PTS, FEAT), cond_pos.reshape(-1), num_segments=block_count)

        def accumulate(running, blocked):
            x_block, cot_block = blocked
            preact, hidden, unused = features_of(x_block, weight_in16, bias_now, weight_out16)
            grad_in, grad_bias, grad_out = mlp_backward(x_block, preact, hidden, cot_block, weight_out16)
            return ((running[0] + grad_in, running[1] + grad_bias, running[2] + grad_out), None)
        zero_grads = (jnp.zeros(params[0].shape, jnp.float32), jnp.zeros(params[1].shape, jnp.float32), jnp.zeros(params[2].shape, jnp.float32))
        gradients, unused = lax.scan(accumulate, zero_grads, (x_blocks, total_cot))
        squares = jnp.sum(gradients[0] * gradients[0]) + jnp.sum(gradients[1] * gradients[1]) + jnp.sum(gradients[2] * gradients[2])
        scaling = step_length / jnp.sqrt(squares + epsilon)
        params = (params[0] - scaling * gradients[0], params[1] - scaling * gradients[1], params[2] - scaling * gradients[2])
    return (white_all.reshape(-1), params[0], params[1], params[2])
```

```python
import functools
import jax, jax.numpy as jnp
from jax import lax
from jax.experimental import pallas as pl
from jax.experimental.pallas import tpu as pltpu
f32=jnp.float32; bf16=jnp.bfloat16
PTS=128; HID=512; FEAT=128; ROWS=136

def split(x):
    hi=x.astype(bf16)
    return hi,(x-hi.astype(f32)).astype(bf16)

def mm(a,b):
    return lax.dot_general(a,b,(((1,),(0,)),((),())),preferred_element_type=f32)

def mm_t(a,b):
    return lax.dot_general(a,b,(((1,),(1,)),((),())),preferred_element_type=f32)

def t_mm(a,b):
    return lax.dot_general(a,b,(((0,),(0,)),((),())),preferred_element_type=f32)

def mm3(a,b):
    ah,al=split(a); bh,bl=split(b)
    return mm(jnp.concatenate([ah,al,ah],1),jnp.concatenate([bh,bh,bl],0))

def mm3_t(a,b):
    ah,al=split(a); bh,bl=split(b)
    return mm_t(jnp.concatenate([ah,al,ah],1),jnp.concatenate([bh,bh,bl],1))

def sweep(mats, GS=16):
    nb=len(mats); H=GS//8
    sub=lax.broadcasted_iota(jnp.int32,(8,128),0); lane8=lax.broadcasted_iota(jnp.int32,(8,128),1)
    lane=lax.broadcasted_iota(jnp.int32,(128,128),1)
    bc=lambda x,s: jnp.broadcast_to(x[s:s+1,:],(8,128))
    A=[m[0] for m in mats]; Y=[m[1] for m in mats]; W=[[] for _ in mats]
    for g in range(128//GS):
        c=GS*g
        pre=[]; a=[];y=[];w=[];cols=[]
        for b in range(nb):
            pre.append(split(A[b]))
            a.append([A[b][c+8*h:c+8*h+8,:] for h in range(H)])
            y.append([Y[b][c+8*h:c+8*h+8,:] for h in range(H)])
            w.append([y[b][h] for h in range(H)])
            cols.append([[jnp.broadcast_to(a[b][h][:,c+j:c+j+1],(8,128)) for h in range(H)] for j in range(GS)])
        for k in range(GS):
            h0,s=k//8,k%8
            for b in range(nb):
                d=bc(cols[b][k][h0],s); inv=1.0/d
                t=[cols[b][k][h]*inv for h in range(H)]
                t[h0]=jnp.where(sub==s,1.0-inv,t[h0])
                for h in range(H):
                    e=jnp.where(sub==s,1.0,0.0) if h==h0 else 0.0
                    a[b][h]=jnp.where(lane8==c+k,e,a[b][h])
                ra=bc(a[b][h0],s); ry=bc(y[b][h0],s)
                w[b][h0]=jnp.where(sub==s,ry*lax.rsqrt(d),w[b][h0])
                for j in range(k+1,GS):
                    rj=bc(cols[b][j][h0],s)
                    for h in range(H): cols[b][j][h]=cols[b][j][h]-t[h]*rj
                for h in range(H):
                    a[b][h]=a[b][h]-t[h]*ra
                    y[b][h]=y[b][h]-t[h]*ry
        for b in range(nb):
            Gr=jnp.concatenate([jnp.concatenate(a[b],0),jnp.concatenate(y[b],0)],1)
            gh,gl=split(Gr)
            z=lambda n: jnp.zeros((n,256),bf16)
            emb=lambda x: jnp.concatenate(([z(c)] if c else [])+[x]+([z(128-c-GS)] if 128-c-GS else []),0)
            eh=emb(gh); el=emb(gl); ah,al=pre[b]
            U=mm(jnp.concatenate([ah,al,ah],1),jnp.concatenate([eh,eh,el],0))
            inc=(lane>=c)&(lane<c+GS)
            An=jnp.where(inc,0.0,A[b])-U[:,:128]; Yn=Y[b]-U[:,128:]
            put=lambda full,part: jnp.concatenate(([full[:c]] if c else [])+[part]+([full[c+GS:]] if c+GS<128 else []),0)
            A[b]=put(An,Gr[:,:128]); Y[b]=put(Yn,Gr[:,128:])
            W[b]+=w[b]
    return [(A[b],Y[b],jnp.concatenate(W[b],0)) for b in range(nb)]

def local_kernel(weight, allx_ref, win_ref, bin_ref, wout_ref, w_out, pk_out,
                 x_s, hid_s, slope_s, f_s, e_s, a_s, y_s, cot_s):
    NB=2
    win16=win_ref[...].astype(bf16); wout16=wout_ref[...].astype(bf16); bias=bin_ref[...]
    eye=(lax.broadcasted_iota(jnp.int32,(128,128),0)==lax.broadcasted_iota(jnp.int32,(128,128),1))
    ones=jnp.ones((128,128),bf16)
    for i in range(6):
        b,j=divmod(i,3)
        blk=allx_ref[i]
        x=blk[:128,:]
        x_s[pl.ds(128*i,128),:]=x
        yrow=blk[128:136,:].astype(f32)[0:1,:]
        diag=jnp.where(eye,jnp.broadcast_to(yrow,(128,128)),0.0).astype(bf16)
        y_s[b,j]=mm(diag,ones)
        pre=mm(x,win16)+bias
        s=1.0/(1.0+jnp.exp(-pre))
        hid=(pre*s).astype(bf16)
        slope_s[pl.ds(128*i,128),:]=s*(1.0+pre*(1.0-s))
        hid_s[pl.ds(128*i,128),:]=hid
        f_s[pl.ds(128*i,128),:]=mm(hid,wout16).astype(bf16)
    for b in range(NB):
        F=f_s[pl.ds(384*b,384),:]; Ff=F.astype(f32)
        FF=Ff*Ff
        sqc=jnp.sum(FF,axis=1,keepdims=True)
        fh,fl=split(FF)
        o8=jnp.ones((8,128),bf16)
        sqr=(mm_t(o8,fh)+mm_t(o8,fl))[0:1,:]
        cross=mm_t(F,F)
        E=jnp.exp((sqc+sqr-2.0*cross)*(-2.0/FEAT))
        for i in range(3):
            for j in range(3):
                t=E[128*i:128*i+128,128*j:128*j+128]
                e_s[b,i,j]=t
                a_s[b,i,j]=jnp.where(eye,t+0.5,t) if i==j else t
    r=sweep([(a_s[b,0,0],y_s[b,0]) for b in range(NB)])
    for b in range(NB):
        D,Y1,_=r[b]
        Hm=mm3(D,jnp.concatenate([a_s[b,0,1],a_s[b,0,2]],1))
        R=jnp.concatenate([Hm,Y1],1)
        L=jnp.concatenate([a_s[b,1,0],a_s[b,2,0]],0)
        U=mm3(L,R)
        a_s[b,1,1]=a_s[b,1,1]-U[:128,:128]
        a_s[b,1,2]=a_s[b,1,2]-U[:128,128:256]
        a_s[b,2,1]=a_s[b,2,1]-U[128:,:128]
        a_s[b,2,2]=a_s[b,2,2]-U[128:,128:256]
        y_s[b,1]=y_s[b,1]-U[:128,256:]
        y_s[b,2]=y_s[b,2]-U[128:,256:]
        a_s[b,0,1]=Hm[:,:128]; a_s[b,0,2]=Hm[:,128:]; y_s[b,0]=Y1
    r=sweep([(a_s[b,1,1],y_s[b,1]) for b in range(NB)])
    for b in range(NB):
        D,Y2,_=r[b]
        Hb=mm3(D,a_s[b,1,2])
        L=jnp.concatenate([a_s[b,0,1],a_s[b,2,1]],0)
        U=mm3(L,jnp.concatenate([Hb,Y2],1))
        a_s[b,0,2]=a_s[b,0,2]-U[:128,:128]
        a_s[b,1,2]=Hb
        a_s[b,2,2]=a_s[b,2,2]-U[128:,:128]
        y_s[b,0]=y_s[b,0]-U[:128,128:]
        y_s[b,1]=Y2
        y_s[b,2]=y_s[b,2]-U[128:,128:]
    r=sweep([(a_s[b,2,2],y_s[b,2]) for b in range(NB)])
    torow=lambda Y: jnp.sum(jnp.where(eye,Y,0.0),axis=0,keepdims=True)
    for b in range(NB):
        D,ab,W=r[b]
        w_out[pl.ds(b,1),:]=torow(W)
        G=jnp.concatenate([a_s[b,0,2],a_s[b,1,2]],0)
        v=jnp.concatenate([y_s[b,0],y_s[b,1]],0)
        Pa=mm3(G,jnp.concatenate([D,ab],1))
        Pm=Pa[:,:128]; ac=v-Pa[:,128:]
        PT=mm3_t(D,G)
        Z=mm3_t(Pm,G)
        abr=torow(ab); acr=[torow(ac[:128]),torow(ac[128:])]; vr=[torow(v[:128]),torow(v[128:])]
        acs=[ac[:128],ac[128:]]; vs=[v[:128],v[128:]]
        rows=[]
        for i in range(3):
            row=[]
            for j in range(3):
                if i<2 and j<2: gm=Z[128*i:128*i+128,128*j:128*j+128]-acs[i]*acr[j]+vs[i]*vr[j]
                elif i<2: gm=-Pm[128*i:128*i+128,:]-acs[i]*abr
                elif j<2: gm=-PT[:,128*j:128*j+128]-ab*acr[j]
                else: gm=D-ab*abr
                t=0.5*gm*e_s[b,i,j]
                if i==j: t=jnp.where(eye,0.0,t)
                row.append(t)
            rows.append(jnp.concatenate(row,1))
        em=jnp.concatenate(rows,0)
        eh,el=split(em)
        F=f_s[pl.ds(384*b,384),:]
        Fo=jnp.concatenate([F,jnp.ones((384,128),bf16)],1)
        ef=mm(jnp.concatenate([eh,el],1),jnp.concatenate([Fo,Fo],0))
        cot_s[pl.ds(384*b,384),:]=((-8.0*weight/FEAT)*(ef[:,128:]*F.astype(f32)-ef[:,:128])).astype(bf16)
    cot=cot_s[...]
    backed=mm_t(cot,wout16)*slope_s[...]
    gin=t_mm(x_s[...],backed.astype(bf16)).astype(bf16)
    gout=t_mm(cot,hid_s[...]).astype(bf16)
    gb=jnp.sum(backed,axis=0,keepdims=True).astype(bf16)
    gb8=jnp.concatenate([gb[:,128*i:128*i+128] for i in range(4)]+[jnp.zeros((4,128),bf16)],0)
    for i in range(16):
        pk_out[i]=jnp.concatenate([gin[8*i:8*i+8,:],gb8],1)
        pk_out[16+i]=jnp.concatenate([gout[8*i:8*i+8,:],gb8],1)

def local_call(blocks, win, bin_, wout, weight):
    V=pltpu.VMEM
    return pl.pallas_call(
        functools.partial(local_kernel, weight),
        out_shape=(jax.ShapeDtypeStruct((2,128),f32),jax.ShapeDtypeStruct((32,8,640),bf16)),
        in_specs=[pl.BlockSpec(memory_space=V)]*4,
        out_specs=(pl.BlockSpec(memory_space=V),)*2,
        scratch_shapes=[V((768,128),bf16),V((768,512),bf16),V((768,512),f32),V((768,128),bf16),V((2,3,3,128,128),f32),V((2,3,3,128,128),f32),V((2,3,128,128),f32),V((768,128),bf16)],
        name="local_terms",
    )(blocks,win,bin_,wout)


from jax.sharding import PartitionSpec as P

MESH = pl.DeviceIdType.MESH
CHUNKS = 32


def remote(src, dst, send_sem, recv_sem, device):
    return pltpu.make_async_remote_copy(
        src_ref=src, dst_ref=dst, send_sem=send_sem, recv_sem=recv_sem,
        device_id=device, device_id_type=MESH,
    )


def gather_kernel(idx_ref, own_ref, out_ref, buf, send_sem, recv_sem, local_sem):
    me = lax.axis_index("blk")
    here = (me // 8, (me // 2) % 4)
    core = me % 2
    partner = me + 1 - 2 * core
    sign = 1 - 2 * core

    def peer(first, dp, dq):
        p = (here[first] + dp + 4) % 4
        q = (here[1 - first] + dq + 4) % 4
        yy, xx = (p, q) if first == 0 else (q, p)
        return yy * 8 + xx * 2 + core

    barrier = pltpu.get_barrier_semaphore()
    near = [peer(0, 1, 0), peer(0, 3, 0), peer(0, 0, 1), peer(0, 0, 3), partner]
    for dev in near:
        pl.semaphore_signal(barrier, inc=1, device_id={"blk": dev}, device_id_type=MESH)
    pl.semaphore_wait(barrier, len(near))

    sends = []

    def push(src, slot, half, dev, sem):
        cp = remote(src, buf.at[slot, half], send_sem.at[half, sem], recv_sem.at[half, sem], {"blk": dev})
        cp.start()
        sends.append(cp)

    def arrive(slot, half, sem):
        remote(
            buf.at[slot, half], buf.at[slot, half], send_sem.at[half, sem], recv_sem.at[half, sem],
            {"blk": partner},
        ).wait_recv()

    locals_ = []
    for h in range(2):
        cp = pltpu.make_async_copy(own_ref.at[h], buf.at[me, h], local_sem.at[h])
        cp.start()
        locals_.append(cp)

    offs = (0, 1, 3, 2)
    turn = (1, -1, -1, 1)

    def spread(src, slot, half, i):
        first = 1 - half
        push(src, slot, half, peer(first, 0, 1), 3 + 2 * i)
        push(src, slot, half, peer(first, 0, 3), 4 + 2 * i)

    def relay(src, slot, half, i, j):
        push(src, slot, half, partner, 15 + 4 * i + j)

    for h in range(2):
        first = 1 - h
        push(own_ref.at[h], me, h, peer(first, 1, 0), 0)
        push(own_ref.at[h], me, h, peer(first, 3, 0), 1)
    for h in range(2):
        spread(own_ref.at[h], me, h, 0)
        relay(own_ref.at[h], me, h, 0, 0)
    for h in range(2):
        first = 1 - h
        behind, ahead = peer(first, 3, 0), peer(first, 1, 0)
        arrive(behind, h, 0)
        arrive(ahead, h, 1)
        passed = peer(first, 4 - sign, 0)
        push(buf.at[passed, h], passed, h, peer(first, 4 + sign, 0), 2)
        for i, slot in ((1, ahead), (2, behind)):
            spread(buf.at[slot, h], slot, h, i)
            relay(buf.at[slot, h], slot, h, i, 0)

    def second(h, i):
        first = 1 - h
        s_ = turn[i]
        behind, ahead = peer(first, offs[i], 3), peer(first, offs[i], 1)
        arrive(behind, h, 3 + 2 * i)
        arrive(ahead, h, 4 + 2 * i)
        passed = behind if s_ == 1 else ahead
        push(buf.at[passed, h], passed, h, peer(first, 0, s_ % 4), 11 + i)
        relay(buf.at[ahead, h], ahead, h, i, 1)
        relay(buf.at[behind, h], behind, h, i, 3)

    for h in range(2):
        second(h, 0)
    for h in range(2):
        first = 1 - h
        far = peer(first, 2, 0)
        arrive(far, h, 2)
        spread(buf.at[far, h], far, h, 3)
        relay(buf.at[far, h], far, h, 3, 0)
    for i in (1, 2, 3):
        for h in range(2):
            second(h, i)
    for i in range(4):
        for h in range(2):
            far = peer(1 - h, offs[i], 2)
            arrive(far, h, 11 + i)
            relay(buf.at[far, h], far, h, i, 2)
    for i in range(4):
        for h in range(2):
            for j in range(4):
                slot = peer(1 - h, offs[i], (0, 1, 2, 3)[j]) + 1 - 2 * core
                arrive(slot, h, 15 + 4 * i + j)
    for cp in locals_:
        cp.wait()
    for n in range(2):
        out_ref[3 * n + 2] = own_ref[n]
        for j in range(2):
            at = idx_ref[2 * n + j]
            out_ref[3 * n + j] = buf[at // 2, at % 2]
    for cp in sends:
        cp.wait_send()


def gather_call(idx, own):
    V = pltpu.VMEM
    return pl.pallas_call(
        gather_kernel,
        out_shape=jax.ShapeDtypeStruct((6, ROWS, 128), bf16),
        in_specs=[pl.BlockSpec(memory_space=pltpu.SMEM), pl.BlockSpec(memory_space=V)],
        out_specs=pl.BlockSpec(memory_space=V),
        scratch_shapes=[
            V((32, 2, ROWS, 128), bf16),
            pltpu.SemaphoreType.DMA((2, 31)),
            pltpu.SemaphoreType.DMA((2, 31)),
            pltpu.SemaphoreType.DMA((2,)),
        ],
        compiler_params=pltpu.CompilerParams(collective_id=0, has_side_effects=True),
        name="gather_blocks",
    )(idx, own)


def reduce_kernel(pk_ref, win_ref, bin_ref, wout_ref, in_out, bias_out, out_out,
                  rs_buf, part, z_buf, ag_buf, final, rs_send, rs_recv, z_send, z_recv, ag_send, ag_recv):
    me = lax.axis_index("blk")
    z = lax.axis_index("grp")
    barrier = pltpu.get_barrier_semaphore()
    plane = [(me + o) % 32 for o in range(1, 32)]
    column = [(z + o) % 8 for o in range(1, 8)]
    for dev in plane:
        pl.semaphore_signal(barrier, inc=1, device_id={"blk": dev}, device_id_type=MESH)
    for dev in column:
        pl.semaphore_signal(barrier, inc=1, device_id={"grp": dev}, device_id_type=MESH)
    pl.semaphore_wait(barrier, 38)
    sends = []

    def push(src, dst, ss, rs, dev):
        cp = remote(src, dst, ss, rs, dev)
        cp.start()
        sends.append(cp)

    for o, dev in enumerate(plane):
        push(pk_ref.at[dev], rs_buf.at[me], rs_send.at[o], rs_recv.at[o], {"blk": dev})
    rs_buf[me] = pk_ref[me]
    for o in range(31):
        src = (me + 31 - o) % 32
        remote(pk_ref.at[src], rs_buf.at[src], rs_send.at[o], rs_recv.at[o], {"blk": src}).wait_recv()
    acc = rs_buf[0].astype(f32)
    for i in range(1, 32):
        acc = acc + rs_buf[i].astype(f32)
    part[...] = acc.astype(bf16)
    z_buf[z] = acc.astype(bf16)
    for o, dev in enumerate(column):
        push(part, z_buf.at[z], z_send.at[o], z_recv.at[o], {"grp": dev})
    for o in range(7):
        src = (z + 7 - o) % 8
        remote(part, z_buf.at[src], z_send.at[o], z_recv.at[o], {"grp": src}).wait_recv()
    acc = z_buf[0].astype(f32)
    for i in range(1, 8):
        acc = acc + z_buf[i].astype(f32)
    done = acc[:, :512].astype(bf16)
    bias = acc[:4, 512:]
    final[...] = done
    ag_buf[me] = done
    for o, dev in enumerate(plane):
        push(final, ag_buf.at[me], ag_send.at[o], ag_recv.at[o], {"blk": dev})
    for o in range(31):
        src = (me + 31 - o) % 32
        remote(final, ag_buf.at[src], ag_send.at[o], ag_recv.at[o], {"blk": src}).wait_recv()
    total = jnp.zeros((8, 512), f32)
    for i in range(32):
        t = ag_buf[i].astype(f32)
        total = total + t * t
    squares = jnp.sum(total) + jnp.sum(bias * bias)
    scale = 3.0 / jnp.sqrt(jnp.broadcast_to(squares, (1, 1)) + 1e-06)
    bias_out[...] = bin_ref[...] - scale * bias
    for i in range(16):
        in_out[pl.ds(8 * i, 8), :] = win_ref[pl.ds(8 * i, 8), :] - scale * ag_buf[i].astype(f32)
    for q in range(4):
        t = jnp.concatenate([ag_buf[16 + i][:, 128 * q:128 * q + 128].astype(f32) for i in range(16)], 0)
        out_out[pl.ds(128 * q, 128), :] = wout_ref[pl.ds(128 * q, 128), :] - scale * jnp.transpose(t)
    for cp in sends:
        cp.wait_send()


def reduce_call(pk, win, bias, wout):
    V = pltpu.VMEM
    D = pltpu.SemaphoreType.DMA
    return pl.pallas_call(
        reduce_kernel,
        out_shape=(
            jax.ShapeDtypeStruct((128, 512), f32),
            jax.ShapeDtypeStruct((4, 128), f32),
            jax.ShapeDtypeStruct((512, 128), f32),
        ),
        in_specs=[pl.BlockSpec(memory_space=V)] * 4,
        out_specs=(pl.BlockSpec(memory_space=V),) * 3,
        scratch_shapes=[
            V((32, 8, 640), bf16), V((8, 640), bf16), V((8, 8, 640), bf16),
            V((32, 8, 512), bf16), V((8, 512), bf16),
            D((31,)), D((31,)), D((7,)), D((7,)), D((31,)), D((31,)),
        ],
        compiler_params=pltpu.CompilerParams(collective_id=1, has_side_effects=True),
        name="sum_gradients",
    )(pk, win, bias, wout)


def shards(inputs, targets, weight_in, bias_in, weight_out, neighbors, owner_map):
    me = lax.axis_index("blk")
    region = lax.axis_index("grp")
    first = region * 64
    ids = lax.dynamic_slice_in_dim(neighbors, first + 2 * me, 2, 0).reshape(-1)
    idx = jnp.take(owner_map, ids, axis=0) - first
    own = jnp.concatenate(
        [inputs.reshape(2, PTS, 128), jnp.pad(targets.reshape(2, 1, PTS), ((0, 0), (0, 7), (0, 0)))], 1
    )
    blocks = gather_call(idx, own)
    white, packed = local_call(blocks, weight_in, bias_in.reshape(1, -1), weight_out, 1.0 / neighbors.shape[0])
    new_in, new_bias, new_out = reduce_call(packed, weight_in, bias_in.reshape(4, 128), weight_out)
    return (white.reshape(-1), new_in, new_bias.reshape(-1), new_out)


def solution(mesh):
    placed = (P(("grp", "blk"), None), P(("grp", "blk")), P(), P(), P(), P(), P())
    return jax.shard_map(
        shards,
        mesh=mesh,
        in_specs=placed,
        out_specs=(P(("grp", "blk")), P(), P(), P()),
        check_vma=False,
    )
```

```python
import functools
import jax, jax.numpy as jnp
from jax import lax
from jax.experimental import pallas as pl
from jax.experimental.pallas import tpu as pltpu
from jax.sharding import PartitionSpec as P
f32=jnp.float32; bf16=jnp.bfloat16
PTS=128; HID=512; FEAT=128; ROWS=136

def split(x):
    hi=x.astype(bf16)
    return hi,(x-hi.astype(f32)).astype(bf16)

def mm(a,b):
    return lax.dot_general(a,b,(((1,),(0,)),((),())),preferred_element_type=f32)

def mm_t(a,b):
    return lax.dot_general(a,b,(((1,),(1,)),((),())),preferred_element_type=f32)

def t_mm(a,b):
    return lax.dot_general(a,b,(((0,),(0,)),((),())),preferred_element_type=f32)

def mm3(a,b):
    ah,al=split(a); bh,bl=split(b)
    return mm(jnp.concatenate([ah,al,ah],1),jnp.concatenate([bh,bh,bl],0))

def mm3_t(a,b):
    ah,al=split(a); bh,bl=split(b)
    return mm_t(jnp.concatenate([ah,al,ah],1),jnp.concatenate([bh,bh,bl],1))

LOW, HIGH, DOUBLINGS = 0.5, 128.5, 6


def inverses(mats):
    eye = lax.broadcasted_iota(jnp.int32, (128, 128), 0) == lax.broadcasted_iota(jnp.int32, (128, 128), 1)
    ident = jnp.where(eye, 1.0, 0.0)
    centre = (HIGH + LOW) / (HIGH - LOW)
    first = 2.0 / (HIGH + LOW)
    res = [ident - first * m for m in mats]
    inv = [first * ident for m in mats]
    tau = centre
    for step in range(DOUBLINGS):
        twice = 2.0 * tau * tau - 1.0
        gain = 2.0 * tau * tau / twice
        shift = 1.0 / twice
        if step == 0:
            prods = [mm3(r, r) for r in res]
            inv = [(gain * first) * (ident + r) for r in res]
            res = [gain * p - shift * ident for p in prods]
        elif step < DOUBLINGS - 1:
            prods = [mm3(jnp.concatenate([r, x], 0), r) for r, x in zip(res, inv)]
            inv = [gain * (x + p[128:]) for x, p in zip(inv, prods)]
            res = [gain * p[:128] - shift * ident for p in prods]
        else:
            inv = [gain * (x + mm3(x, r)) for x, r in zip(inv, res)]
        tau = twice
    left = [ident - mm3(m, x) for m, x in zip(mats, inv)]
    return [x + mm3(x, r) for x, r in zip(inv, left)]


MESH = pl.DeviceIdType.MESH
V = pltpu.VMEM


def eliminate_group(mats, rows):
    nb = len(mats)
    sub = lax.broadcasted_iota(jnp.int32, (8, 128), 0)
    spread = lambda x, s: jnp.broadcast_to(x[s:s + 1, :], (8, 128))
    a = [[m[8 * h:8 * h + 8, :] for h in range(2)] for m in mats]
    y = [[r[8 * h:8 * h + 8, :] for h in range(2)] for r in rows]
    w = [[r[8 * h:8 * h + 8, :] for h in range(2)] for r in rows]
    cols = [[[jnp.broadcast_to(a[b][h][:, j:j + 1], (8, 128)) for h in range(2)] for j in range(16)] for b in range(nb)]
    for k in range(16):
        h0, s = divmod(k, 8)
        for b in range(nb):
            d = spread(cols[b][k][h0], s)
            inv = 1.0 / d
            t = [cols[b][k][h] * inv for h in range(2)]
            t[h0] = jnp.where(sub == s, 1.0 - inv, t[h0])
            ra = spread(a[b][h0], s)
            ry = spread(y[b][h0], s)
            w[b][h0] = jnp.where(sub == s, ry * lax.rsqrt(d), w[b][h0])
            for j in range(k + 1, 16):
                rj = spread(cols[b][j][h0], s)
                for h in range(2):
                    cols[b][j][h] = cols[b][j][h] - t[h] * rj
            for h in range(2):
                a[b][h] = a[b][h] - t[h] * ra
                y[b][h] = y[b][h] - t[h] * ry
    out = []
    for b in range(nb):
        done = jnp.concatenate([jnp.concatenate(a[b], 0), jnp.concatenate(y[b], 0)], 1)
        dh, dl = split(done)
        pad = jnp.zeros((112, 256), bf16)
        dh = jnp.concatenate([dh, pad], 0)
        dl = jnp.concatenate([dl, pad], 0)
        ah, al = split(mats[b])
        upd = mm(jnp.concatenate([ah, al, ah], 1), jnp.concatenate([dh, dh, dl], 0))
        rest = jnp.concatenate([mats[b][16:] - upd[16:, :128], done[:, :128]], 0)
        side = jnp.concatenate([rows[b][16:] - upd[16:, 128:], done[:, 128:]], 0)
        out.append((pltpu.roll(rest, 112, 1), side, jnp.concatenate(w[b], 0)))
    return out


def main_kernel(weight, nb_ref, om_ref, x_ref, t_ref, win_ref, bin_ref, wout_ref,
                w_out, tot_out, bias_out,
                buf, give, take, x_s, hid_s, slope_s, f_s, e_s, a_s, y_s, cot_s, sw_s, sr_s, ww_s,
                pk, rs_buf, part, z_buf, ag_buf,
                g_send, g_recv, d_sem, rs_send, rs_recv, z_send, z_recv, ag_send, ag_recv):
    me = lax.axis_index("blk")
    z = lax.axis_index("grp")
    here = (me // 8, (me // 2) % 4)
    core = me % 2
    partner = me + 1 - 2 * core
    chip = me // 2

    def chip_at(first, dp, dq):
        p = (here[first] + dp) % 4
        q = (here[1 - first] + dq) % 4
        return p * 4 + q if first == 0 else q * 4 + p

    def peer(first, dp, dq):
        return 2 * chip_at(first, dp, dq) + core

    sends = []

    def push(src, dst, ss, rs, dev):
        cp = pltpu.make_async_remote_copy(
            src_ref=src, dst_ref=dst, send_sem=ss, recv_sem=rs, device_id=dev, device_id_type=MESH
        )
        cp.start()
        sends.append(cp)

    def arrive(dst, ss, rs, dev):
        pltpu.make_async_remote_copy(
            src_ref=dst, dst_ref=dst, send_sem=ss, recv_sem=rs, device_id=dev, device_id_type=MESH
        ).wait_recv()

    barrier = pltpu.get_barrier_semaphore()
    near = [{"blk": peer(f, d, 0)} for f in range(2) for d in (1, 2, 3)] + [{"blk": partner}]
    column = [(z + o) % 8 for o in range(1, 8)]
    greeted = near + [{"grp": d} for d in column]
    for dev in greeted:
        pl.semaphore_signal(barrier, inc=1, device_id=dev, device_id_type=MESH)

    for h in range(2):
        buf[chip, h, pl.ds(0, 128), :] = x_ref[pl.ds(128 * h, 128), :]
        buf[chip, h, pl.ds(128, 8), :] = jnp.broadcast_to(t_ref[pl.ds(h, 1), :].astype(f32), (8, 128)).astype(bf16)
    pl.semaphore_wait(barrier, len(greeted))

    def fan(h, at, axis, base):
        for n, d in ((2, 2), (0, 1), (1, 3)):
            dev = peer(axis, d, 0)
            push(buf.at[at, h], buf.at[at, h], g_send.at[h, base + n], g_recv.at[h, base + n], {"blk": dev})

    def got(h, at, sem):
        arrive(buf.at[at, h], g_send.at[h, sem], g_recv.at[h, sem], {"blk": partner})

    firsts = (1, 0)
    for h in range(2):
        fan(h, chip, firsts[h], 0)
    for h in range(2):
        fan(h, chip, 1 - firsts[h], 3)

    win16 = win_ref[...].astype(bf16)
    wout16 = wout_ref[...].astype(bf16)
    bias = bin_ref[...]
    eye = lax.broadcasted_iota(jnp.int32, (128, 128), 0) == lax.broadcasted_iota(jnp.int32, (128, 128), 1)
    ones = jnp.ones((128, 128), bf16)

    def forward(i, blk):
        x = blk[:128, :]
        x_s[pl.ds(128 * i, 128), :] = x
        yrow = blk[128:136, :].astype(f32)[0:1, :]
        diag = jnp.where(eye, jnp.broadcast_to(yrow, (128, 128)), 0.0).astype(bf16)
        y_s[i] = mm(diag, ones)
        pre = mm(x, win16) + bias
        s = 1.0 / (1.0 + jnp.exp(-pre))
        hid = (pre * s).astype(bf16)
        slope_s[pl.ds(128 * i, 128), :] = s * (1.0 + pre * (1.0 - s))
        hid_s[pl.ds(128 * i, 128), :] = hid
        f_s[pl.ds(128 * i, 128), :] = mm(hid, wout16).astype(bf16)

    origin = {0: 3, 1: 1, 2: 2}
    for n in (0, 1, 2):
        for h in range(2):
            at = chip_at(firsts[h], origin[n], 0)
            got(h, at, n)
            fan(h, at, 1 - firsts[h], 6 + 3 * n)
    for h in range(2):
        forward(3 * h + 2, buf[chip, h])
    for k in range(4):
        for n in (0, 1, 2):
            for h in range(2):
                dp = 0 if k == 0 else origin[k - 1]
                got(h, chip_at(firsts[h], dp, origin[n]), 3 + 3 * k + n)

    base = 64 * z

    def wanted(dev, n, j):
        pos = om_ref[nb_ref[j, base + 2 * dev + n]] % 64
        return pos // 4, (pos // 2) % 2, pos % 2

    for n in range(2):
        for j in range(2):
            at, unused, half = wanted(partner, n, j)
            give[2 * n + j] = buf[at, half]
    push(give, take, d_sem.at[0], d_sem.at[1], {"blk": partner})
    mine = []
    for n in range(2):
        for j in range(2):
            at, owner, half = wanted(me, n, j)
            mine.append((buf[at, half], owner))
    arrive(take, d_sem.at[0], d_sem.at[1], {"blk": partner})
    for n in range(2):
        for j in range(2):
            blk, owner = mine[2 * n + j]
            same = jnp.broadcast_to(owner, (ROWS, 128)) == core
            forward(3 * n + j, jnp.where(same, blk.astype(f32), take[2 * n + j].astype(f32)).astype(bf16))

    NB = 2
    for b in range(NB):
        F = f_s[pl.ds(384 * b, 384), :]
        Ff = F.astype(f32)
        FF = Ff * Ff
        sqc = jnp.sum(FF, axis=1, keepdims=True)
        fh, fl = split(FF)
        o8 = jnp.ones((8, 128), bf16)
        sqr = (mm_t(o8, fh) + mm_t(o8, fl))[0:1, :]
        cross = mm_t(F, F)
        E = jnp.exp((sqc + sqr - 2.0 * cross) * (-2.0 / FEAT))
        for i in range(3):
            for j in range(3):
                t = E[128 * i:128 * i + 128, 128 * j:128 * j + 128]
                e_s[b, i, j] = t
                a_s[b, i, j] = jnp.where(eye, t + 0.5, t) if i == j else t
    Y = lambda b, i: 3 * b + i
    r = inverses([a_s[b, 0, 0] for b in range(NB)])
    for b in range(NB):
        R = mm3(r[b], jnp.concatenate([a_s[b, 0, 1], a_s[b, 0, 2], y_s[Y(b, 0)]], 1))
        U = mm3(jnp.concatenate([a_s[b, 1, 0], a_s[b, 2, 0]], 0), R)
        a_s[b, 1, 1] = a_s[b, 1, 1] - U[:128, :128]
        a_s[b, 1, 2] = a_s[b, 1, 2] - U[:128, 128:256]
        a_s[b, 2, 1] = a_s[b, 2, 1] - U[128:, :128]
        a_s[b, 2, 2] = a_s[b, 2, 2] - U[128:, 128:256]
        y_s[Y(b, 1)] = y_s[Y(b, 1)] - U[:128, 256:]
        y_s[Y(b, 2)] = y_s[Y(b, 2)] - U[128:, 256:]
        a_s[b, 0, 1] = R[:, :128]
        a_s[b, 0, 2] = R[:, 128:256]
        y_s[Y(b, 0)] = R[:, 256:]
    r = inverses([a_s[b, 1, 1] for b in range(NB)])
    for b in range(NB):
        R = mm3(r[b], jnp.concatenate([a_s[b, 1, 2], y_s[Y(b, 1)]], 1))
        U = mm3(jnp.concatenate([a_s[b, 0, 1], a_s[b, 2, 1]], 0), R)
        a_s[b, 0, 2] = a_s[b, 0, 2] - U[:128, :128]
        a_s[b, 1, 2] = R[:, :128]
        a_s[b, 2, 2] = a_s[b, 2, 2] - U[128:, :128]
        y_s[Y(b, 0)] = y_s[Y(b, 0)] - U[:128, 128:]
        y_s[Y(b, 1)] = R[:, 128:]
        y_s[Y(b, 2)] = y_s[Y(b, 2)] - U[128:, 128:]
    r = inverses([a_s[b, 2, 2] for b in range(NB)])
    torow = lambda m: jnp.sum(jnp.where(eye, m, 0.0), axis=0, keepdims=True)
    for b in range(NB):
        D = r[b]
        sw_s[b] = a_s[b, 2, 2]
        sr_s[b] = y_s[Y(b, 2)]
        ab = mm3(D, y_s[Y(b, 2)])
        G = jnp.concatenate([a_s[b, 0, 2], a_s[b, 1, 2]], 0)
        v = jnp.concatenate([y_s[Y(b, 0)], y_s[Y(b, 1)]], 0)
        Pa = mm3(G, jnp.concatenate([D, ab], 1))
        Pm = Pa[:, :128]
        ac = v - Pa[:, 128:]
        PT = mm3_t(D, G)
        Z = mm3_t(Pm, G)
        abr = torow(ab)
        acr = [torow(ac[:128]), torow(ac[128:])]
        vr = [torow(v[:128]), torow(v[128:])]
        acs = [ac[:128], ac[128:]]
        vs = [v[:128], v[128:]]
        rows = []
        for i in range(3):
            row = []
            for j in range(3):
                if i < 2 and j < 2:
                    gm = Z[128 * i:128 * i + 128, 128 * j:128 * j + 128] - acs[i] * acr[j] + vs[i] * vr[j]
                elif i < 2:
                    gm = -Pm[128 * i:128 * i + 128, :] - acs[i] * abr
                elif j < 2:
                    gm = -PT[:, 128 * j:128 * j + 128] - ab * acr[j]
                else:
                    gm = D - ab * abr
                t = 0.5 * gm * e_s[b, i, j]
                if i == j:
                    t = jnp.where(eye, 0.0, t)
                row.append(t)
            rows.append(jnp.concatenate(row, 1))
        eh, el = split(jnp.concatenate(rows, 0))
        F = f_s[pl.ds(384 * b, 384), :]
        Fo = jnp.concatenate([F, jnp.ones((384, 128), bf16)], 1)
        ef = mm(jnp.concatenate([eh, el], 1), jnp.concatenate([Fo, Fo], 0))
        cot_s[pl.ds(384 * b, 384), :] = ((-8.0 * weight / FEAT) * (ef[:, 128:] * F.astype(f32) - ef[:, :128])).astype(bf16)
    cot = cot_s[...]
    backed = mm_t(cot, wout16) * slope_s[...]
    gin = t_mm(x_s[...], backed.astype(bf16)).astype(bf16)
    gout = t_mm(cot, hid_s[...]).astype(bf16)
    gb = jnp.sum(backed, axis=0, keepdims=True).astype(bf16)
    gb8 = jnp.concatenate([gb[:, 128 * i:128 * i + 128] for i in range(4)] + [jnp.zeros((4, 128), bf16)], 0)
    for i in range(16):
        pk[i] = jnp.concatenate([gin[8 * i:8 * i + 8, :], gb8], 1)
        pk[16 + i] = jnp.concatenate([gout[8 * i:8 * i + 8, :], gb8], 1)

    plane = [(me + o) % 32 for o in range(1, 32)]
    for o, dev in enumerate(plane):
        push(pk.at[dev], rs_buf.at[me], rs_send.at[o], rs_recv.at[o], {"blk": dev})
    rs_buf[me] = pk[me]

    def sweep_groups(start, count):
        def step(i, carry):
            res = eliminate_group([sw_s[b] for b in range(NB)], [sr_s[b] for b in range(NB)])
            for b in range(NB):
                sw_s[b] = res[b][0]
                sr_s[b] = res[b][1]
                ww_s[b, start + i] = res[b][2]
            return carry
        lax.fori_loop(0, count, step, 0)

    sweep_groups(0, 3)
    for o in range(31):
        src = (me + 31 - o) % 32
        arrive(rs_buf.at[src], rs_send.at[o], rs_recv.at[o], {"blk": partner})
    acc = rs_buf[0].astype(f32)
    for i in range(1, 32):
        acc = acc + rs_buf[i].astype(f32)
    part[...] = acc.astype(bf16)
    z_buf[z] = acc.astype(bf16)
    for o, dev in enumerate(column):
        push(part, z_buf.at[z], z_send.at[o], z_recv.at[o], {"grp": dev})
    sweep_groups(3, 2)
    for o in range(7):
        src = (z + 7 - o) % 8
        arrive(z_buf.at[src], z_send.at[o], z_recv.at[o], {"blk": partner})
    acc = z_buf[0].astype(f32)
    for i in range(1, 8):
        acc = acc + z_buf[i].astype(f32)
    ag_buf[me] = acc[:, :512].astype(bf16)
    bias_out[...] = acc[:, 512:]
    for o, dev in enumerate(plane):
        push(ag_buf.at[me], ag_buf.at[me], ag_send.at[o], ag_recv.at[o], {"blk": dev})
    sweep_groups(5, 3)
    for b in range(NB):
        w_out[pl.ds(b, 1), :] = torow(jnp.concatenate([ww_s[b, g] for g in range(8)], 0))
    for o in range(31):
        src = (me + 31 - o) % 32
        arrive(ag_buf.at[src], ag_send.at[o], ag_recv.at[o], {"blk": partner})
    tot_out[...] = ag_buf[...]
    for cp in sends:
        cp.wait_send()


def main_call(nb, om, x, t, win, bin_, wout, weight):
    D = pltpu.SemaphoreType.DMA
    smem = pl.BlockSpec(memory_space=pltpu.SMEM)
    vmem = pl.BlockSpec(memory_space=V)
    return pl.pallas_call(
        functools.partial(main_kernel, weight),
        out_shape=(
            jax.ShapeDtypeStruct((2, 128), f32),
            jax.ShapeDtypeStruct((32, 8, 512), bf16),
            jax.ShapeDtypeStruct((8, 128), f32),
        ),
        in_specs=[smem, smem] + [vmem] * 5,
        out_specs=(vmem,) * 3,
        scratch_shapes=[
            V((16, 2, ROWS, 128), bf16), V((4, ROWS, 128), bf16), V((4, ROWS, 128), bf16),
            V((768, 128), bf16), V((768, 512), bf16), V((768, 512), f32), V((768, 128), bf16),
            V((2, 3, 3, 128, 128), f32), V((2, 3, 3, 128, 128), f32), V((6, 128, 128), f32), V((768, 128), bf16),
            V((2, 128, 128), f32), V((2, 128, 128), f32), V((2, 8, 16, 128), f32),
            V((32, 8, 640), bf16), V((32, 8, 640), bf16), V((8, 640), bf16), V((8, 8, 640), bf16), V((32, 8, 512), bf16),
            D((2, 15)), D((2, 15)), D((2,)), D((31,)), D((31,)), D((7,)), D((7,)), D((31,)), D((31,)),
        ],
        compiler_params=pltpu.CompilerParams(collective_id=0, has_side_effects=True),
        name="gradient_step",
    )(nb, om, x, t, win, bin_, wout)


def update_kernel(tot_ref, sum_ref, w_ref, win_ref, bin_ref, wout_ref, w_out, in_out, bias_out, out_out):
    bias = sum_ref[0:4, :]
    total = jnp.zeros((8, 512), f32)
    for i in range(32):
        t = tot_ref[i].astype(f32)
        total = total + t * t
    squares = jnp.sum(total) + jnp.sum(bias * bias)
    scale = 3.0 / jnp.sqrt(jnp.broadcast_to(squares, (1, 1)) + 1e-06)
    w_out[...] = w_ref[...]
    bias_out[...] = bin_ref[...] - scale * bias
    for i in range(16):
        in_out[pl.ds(8 * i, 8), :] = win_ref[pl.ds(8 * i, 8), :] - scale * tot_ref[i].astype(f32)
    for q in range(4):
        t = jnp.concatenate([tot_ref[16 + i][:, 128 * q:128 * q + 128].astype(f32) for i in range(16)], 0)
        out_out[pl.ds(128 * q, 128), :] = wout_ref[pl.ds(128 * q, 128), :] - scale * jnp.transpose(t)


def update_call(tot, total_bias, white, win, bias, wout):
    vmem = pl.BlockSpec(memory_space=V)
    return pl.pallas_call(
        update_kernel,
        out_shape=(
            jax.ShapeDtypeStruct((2, 128), f32),
            jax.ShapeDtypeStruct((128, 512), f32),
            jax.ShapeDtypeStruct((4, 128), f32),
            jax.ShapeDtypeStruct((512, 128), f32),
        ),
        in_specs=[vmem] * 6,
        out_specs=(vmem,) * 4,
        name="update_weights",
    )(tot, total_bias, white, win, bias, wout)


def shards(inputs, targets, weight_in, bias_in, weight_out, neighbors, owner_map):
    white, tot, total_bias = main_call(
        neighbors.T, owner_map, inputs, targets.reshape(2, PTS), weight_in, bias_in.reshape(1, -1), weight_out,
        1.0 / neighbors.shape[0],
    )
    white, new_in, new_bias, new_out = update_call(
        tot, total_bias, white, weight_in, bias_in.reshape(4, 128), weight_out
    )
    return (white.reshape(-1), new_in, new_bias.reshape(-1), new_out)


def solution(mesh):
    placed = (P(("grp", "blk"), None), P(("grp", "blk")), P(), P(), P(), P(), P())
    return jax.shard_map(
        shards,
        mesh=mesh,
        in_specs=placed,
        out_specs=(P(("grp", "blk")), P(), P(), P()),
        check_vma=False,
    )
```

```python
import functools
import jax, jax.numpy as jnp
from jax import lax
from jax.experimental import pallas as pl
from jax.experimental.pallas import tpu as pltpu
from jax.sharding import PartitionSpec as P
f32=jnp.float32; bf16=jnp.bfloat16
PTS=128; HID=512; FEAT=128; ROWS=136

def split(x):
    hi=x.astype(bf16)
    return hi,(x-hi.astype(f32)).astype(bf16)

def mm(a,b):
    return lax.dot_general(a,b,(((1,),(0,)),((),())),preferred_element_type=f32)

def mm_t(a,b):
    return lax.dot_general(a,b,(((1,),(1,)),((),())),preferred_element_type=f32)

def t_mm(a,b):
    return lax.dot_general(a,b,(((0,),(0,)),((),())),preferred_element_type=f32)

def mm3(a,b):
    ah,al=split(a); bh,bl=split(b); n=b.shape[1]
    out=mm(jnp.concatenate([ah,al],1),jnp.concatenate([jnp.concatenate([bh,bl],1),jnp.concatenate([bh,jnp.zeros_like(bl)],1)],0))
    return out[:,:n]+out[:,n:]

def mm3_t(a,b):
    ah,al=split(a); bh,bl=split(b)
    return mm_t(jnp.concatenate([ah,al,ah],1),jnp.concatenate([bh,bh,bl],1))

LOW, HIGH, DOUBLINGS = 0.5, 128.5, 6


def inverses(mats):
    eye = lax.broadcasted_iota(jnp.int32, (128, 128), 0) == lax.broadcasted_iota(jnp.int32, (128, 128), 1)
    ident = jnp.where(eye, 1.0, 0.0)
    centre = (HIGH + LOW) / (HIGH - LOW)
    first = 2.0 / (HIGH + LOW)
    res = [ident - first * m for m in mats]
    inv = [first * ident for m in mats]
    tau = centre
    for step in range(DOUBLINGS):
        twice = 2.0 * tau * tau - 1.0
        gain = 2.0 * tau * tau / twice
        shift = 1.0 / twice
        if step == 0:
            prods = [mm3(r, r) for r in res]
            inv = [(gain * first) * (ident + r) for r in res]
            res = [gain * p - shift * ident for p in prods]
        elif step < DOUBLINGS - 1:
            prods = [mm3(jnp.concatenate([r, x], 0), r) for r, x in zip(res, inv)]
            inv = [gain * (x + p[128:]) for x, p in zip(inv, prods)]
            res = [gain * p[:128] - shift * ident for p in prods]
        else:
            inv = [gain * (x + mm3(x, r)) for x, r in zip(inv, res)]
        tau = twice
    left = [ident - mm3(m, x) for m, x in zip(mats, inv)]
    return [x + mm3(x, r) for x, r in zip(inv, left)]


MESH = pl.DeviceIdType.MESH
MAIN_VMEM = 24 * 1024 * 1024
V = pltpu.VMEM


def eliminate_group(mats, rows):
    nb = len(mats)
    sub = lax.broadcasted_iota(jnp.int32, (8, 128), 0)
    spread = lambda x, s: jnp.broadcast_to(x[s:s + 1, :], (8, 128))
    a = [[m[8 * h:8 * h + 8, :] for h in range(2)] for m in mats]
    y = [[r[8 * h:8 * h + 8, :] for h in range(2)] for r in rows]
    w = [[r[8 * h:8 * h + 8, :] for h in range(2)] for r in rows]
    cols = [[[jnp.broadcast_to(a[b][h][:, j:j + 1], (8, 128)) for h in range(2)] for j in range(16)] for b in range(nb)]
    for k in range(16):
        h0, s = divmod(k, 8)
        for b in range(nb):
            d = spread(cols[b][k][h0], s)
            inv = 1.0 / d
            t = [cols[b][k][h] * inv for h in range(2)]
            t[h0] = jnp.where(sub == s, 1.0 - inv, t[h0])
            ra = spread(a[b][h0], s)
            ry = spread(y[b][h0], s)
            w[b][h0] = jnp.where(sub == s, ry * lax.rsqrt(d), w[b][h0])
            for j in range(k + 1, 16):
                rj = spread(cols[b][j][h0], s)
                for h in range(2):
                    cols[b][j][h] = cols[b][j][h] - t[h] * rj
            for h in range(2):
                a[b][h] = a[b][h] - t[h] * ra
                y[b][h] = y[b][h] - t[h] * ry
    out = []
    for b in range(nb):
        done = jnp.concatenate([jnp.concatenate(a[b], 0), jnp.concatenate(y[b], 0)], 1)
        dh, dl = split(done)
        pad = jnp.zeros((112, 256), bf16)
        dh = jnp.concatenate([dh, pad], 0)
        dl = jnp.concatenate([dl, pad], 0)
        ah, al = split(mats[b])
        upd = mm(jnp.concatenate([ah, al, ah], 1), jnp.concatenate([dh, dh, dl], 0))
        rest = jnp.concatenate([mats[b][16:] - upd[16:, :128], done[:, :128]], 0)
        side = jnp.concatenate([rows[b][16:] - upd[16:, 128:], done[:, 128:]], 0)
        out.append((pltpu.roll(rest, 112, 1), side, jnp.concatenate(w[b], 0)))
    return out


def main_kernel(weight, nb_ref, om_ref, x_ref, t_ref, win_ref, bin_ref, wout_ref,
                w_out, tot_out, bias_out,
                nb_s, om_s, t_s, win_s, bin_s, wout_s, buf, give, take, x_s, hid_s, slope_s, f_s, e_s, a_s, y_s, cot_s, sw_s, sr_s, ww_s,
                pk_a, pk_b, rs_a, rs_b, part_a, part_b, z_a, z_b,
                in_sem, tokens, g_send, g_recv, d_sem, rs_send, rs_recv, z_send, z_recv, ag_send, ag_recv):
    me = lax.axis_index("blk")
    z = lax.axis_index("grp")
    here = (me // 8, (me // 2) % 4)
    core = me % 2
    partner = me + 1 - 2 * core
    chip = me // 2

    def chip_at(first, dp, dq):
        p = (here[first] + dp) % 4
        q = (here[1 - first] + dq) % 4
        return p * 4 + q if first == 0 else q * 4 + p

    def peer(first, dp, dq):
        return 2 * chip_at(first, dp, dq) + core

    sends = []

    def push(src, dst, ss, rs, dev):
        cp = pltpu.make_async_remote_copy(
            src_ref=src, dst_ref=dst, send_sem=ss, recv_sem=rs, device_id=dev, device_id_type=MESH
        )
        cp.start()
        sends.append(cp)

    def arrive(dst, ss, rs, dev):
        pltpu.make_async_remote_copy(
            src_ref=dst, dst_ref=dst, send_sem=ss, recv_sem=rs, device_id=dev, device_id_type=MESH
        ).wait_recv()

    barrier = pltpu.get_barrier_semaphore()
    along = [{"grp": (z + d) % 8} for d in (1, 7)]
    near = [{"blk": peer(f, d, 0)} for f in range(2) for d in (1, 2, 3)] + [{"blk": partner}] + along
    for dev in near:
        pl.semaphore_signal(barrier, inc=1, device_id=dev, device_id_type=MESH)
    fetches = []
    for n, (src, dst) in enumerate((
        (x_ref.at[pl.ds(0, 128)], buf.at[chip, 0, pl.ds(0, 128)]),
        (x_ref.at[pl.ds(128, 128)], buf.at[chip, 1, pl.ds(0, 128)]),
        (t_ref, t_s), (win_ref, win_s), (bin_ref, bin_s), (wout_ref, wout_s), (nb_ref, nb_s), (om_ref, om_s),
    )):
        cp = pltpu.make_async_copy(src, dst, in_sem.at[n])
        cp.start()
        fetches.append(cp)
    for cp in fetches[:3]:
        cp.wait()
    for h in range(2):
        buf[chip, h, pl.ds(128, 8), :] = jnp.broadcast_to(t_s[pl.ds(h, 1), :].astype(f32), (8, 128)).astype(bf16)
    pl.semaphore_wait(barrier, len(near))

    def greet(n):
        if n:
            pl.semaphore_wait(tokens.at[n - 1], 2)
        if n < 3:
            for dev in along:
                pl.semaphore_signal(tokens.at[n], inc=1, device_id=dev, device_id_type=MESH)

    def fan(h, at, axis, base):
        for n, d in ((2, 2), (0, 1), (1, 3)):
            dev = peer(axis, d, 0)
            push(buf.at[at, h], buf.at[at, h], g_send.at[h, base + n], g_recv.at[h, base + n], {"blk": dev})

    def got(h, at, sem):
        arrive(buf.at[at, h], g_send.at[h, sem], g_recv.at[h, sem], {"blk": partner})

    firsts = (1, 0)
    for h in range(2):
        fan(h, chip, firsts[h], 0)
    for h in range(2):
        fan(h, chip, 1 - firsts[h], 3)
    greet(0)
    for cp in fetches[3:]:
        cp.wait()

    win16 = win_s[...].astype(bf16)
    wout16 = wout_s[...].astype(bf16)
    bias = bin_s[...]
    eye = lax.broadcasted_iota(jnp.int32, (128, 128), 0) == lax.broadcasted_iota(jnp.int32, (128, 128), 1)
    ones = jnp.ones((128, 128), bf16)

    def forward(i, blk):
        x = blk[:128, :]
        x_s[pl.ds(128 * i, 128), :] = x
        yrow = blk[128:136, :].astype(f32)[0:1, :]
        diag = jnp.where(eye, jnp.broadcast_to(yrow, (128, 128)), 0.0).astype(bf16)
        y_s[i] = mm(diag, ones)
        pre = mm(x, win16) + bias
        s = 1.0 / (1.0 + jnp.exp(-pre))
        hid = (pre * s).astype(bf16)
        slope_s[pl.ds(128 * i, 128), :] = s * (1.0 + pre * (1.0 - s))
        hid_s[pl.ds(128 * i, 128), :] = hid
        f_s[pl.ds(128 * i, 128), :] = mm(hid, wout16).astype(bf16)

    origin = {0: 3, 1: 1, 2: 2}
    for n in (0, 1, 2):
        for h in range(2):
            at = chip_at(firsts[h], origin[n], 0)
            got(h, at, n)
            fan(h, at, 1 - firsts[h], 6 + 3 * n)
    for h in range(2):
        forward(3 * h + 2, buf[chip, h])
    greet(1)
    for k in range(4):
        for n in (0, 1, 2):
            for h in range(2):
                dp = 0 if k == 0 else origin[k - 1]
                got(h, chip_at(firsts[h], dp, origin[n]), 3 + 3 * k + n)

    greet(2)
    base = 64 * z

    def wanted(dev, n, j):
        pos = om_s[nb_s[j, base + 2 * dev + n]] % 64
        return pos // 4, (pos // 2) % 2, pos % 2

    for n in range(2):
        for j in range(2):
            at, unused, half = wanted(partner, n, j)
            give[2 * n + j] = buf[at, half]
    push(give, take, d_sem.at[0], d_sem.at[1], {"blk": partner})
    mine = []
    for n in range(2):
        for j in range(2):
            at, owner, half = wanted(me, n, j)
            mine.append((buf[at, half], owner))
    greet(3)
    arrive(take, d_sem.at[0], d_sem.at[1], {"blk": partner})
    for n in range(2):
        for j in range(2):
            blk, owner = mine[2 * n + j]
            same = jnp.broadcast_to(owner, (ROWS, 128)) == core
            forward(3 * n + j, jnp.where(same, blk.astype(f32), take[2 * n + j].astype(f32)).astype(bf16))

    NB = 2
    for b in range(NB):
        F = f_s[pl.ds(384 * b, 384), :]
        Ff = F.astype(f32)
        FF = Ff * Ff
        sqc = jnp.sum(FF, axis=1, keepdims=True)
        fh, fl = split(FF)
        o8 = jnp.ones((8, 128), bf16)
        sqr = (mm_t(o8, fh) + mm_t(o8, fl))[0:1, :]
        cross = mm_t(F, F)
        E = jnp.exp((sqc + sqr - 2.0 * cross) * (-2.0 / FEAT))
        for i in range(3):
            for j in range(3):
                t = E[128 * i:128 * i + 128, 128 * j:128 * j + 128]
                e_s[b, i, j] = t
                a_s[b, i, j] = jnp.where(eye, t + 0.5, t) if i == j else t
    Y = lambda b, i: 3 * b + i
    r = inverses([a_s[b, 0, 0] for b in range(NB)])
    for b in range(NB):
        R = mm3(r[b], jnp.concatenate([a_s[b, 0, 1], a_s[b, 0, 2], y_s[Y(b, 0)]], 1))
        U = mm3(jnp.concatenate([a_s[b, 1, 0], a_s[b, 2, 0]], 0), R)
        a_s[b, 1, 1] = a_s[b, 1, 1] - U[:128, :128]
        a_s[b, 1, 2] = a_s[b, 1, 2] - U[:128, 128:256]
        a_s[b, 2, 1] = a_s[b, 2, 1] - U[128:, :128]
        a_s[b, 2, 2] = a_s[b, 2, 2] - U[128:, 128:256]
        y_s[Y(b, 1)] = y_s[Y(b, 1)] - U[:128, 256:]
        y_s[Y(b, 2)] = y_s[Y(b, 2)] - U[128:, 256:]
        a_s[b, 0, 1] = R[:, :128]
        a_s[b, 0, 2] = R[:, 128:256]
        y_s[Y(b, 0)] = R[:, 256:]
    r = inverses([a_s[b, 1, 1] for b in range(NB)])
    for b in range(NB):
        R = mm3(r[b], jnp.concatenate([a_s[b, 1, 2], y_s[Y(b, 1)]], 1))
        U = mm3(jnp.concatenate([a_s[b, 0, 1], a_s[b, 2, 1]], 0), R)
        a_s[b, 0, 2] = a_s[b, 0, 2] - U[:128, :128]
        a_s[b, 1, 2] = R[:, :128]
        a_s[b, 2, 2] = a_s[b, 2, 2] - U[128:, :128]
        y_s[Y(b, 0)] = y_s[Y(b, 0)] - U[:128, 128:]
        y_s[Y(b, 1)] = R[:, 128:]
        y_s[Y(b, 2)] = y_s[Y(b, 2)] - U[128:, 128:]
    r = inverses([a_s[b, 2, 2] for b in range(NB)])
    torow = lambda m: jnp.sum(jnp.where(eye, m, 0.0), axis=0, keepdims=True)
    for b in range(NB):
        D = r[b]
        sw_s[b] = a_s[b, 2, 2]
        sr_s[b] = y_s[Y(b, 2)]
        ab = mm3(D, y_s[Y(b, 2)])
        G = jnp.concatenate([a_s[b, 0, 2], a_s[b, 1, 2]], 0)
        v = jnp.concatenate([y_s[Y(b, 0)], y_s[Y(b, 1)]], 0)
        Pa = mm3(G, jnp.concatenate([D, ab], 1))
        Pm = Pa[:, :128]
        ac = v - Pa[:, 128:]
        PT = mm3_t(D, G)
        Z = mm3_t(Pm, G)
        abr = torow(ab)
        acr = [torow(ac[:128]), torow(ac[128:])]
        vr = [torow(v[:128]), torow(v[128:])]
        acs = [ac[:128], ac[128:]]
        vs = [v[:128], v[128:]]
        rows = []
        for i in range(3):
            row = []
            for j in range(3):
                if i < 2 and j < 2:
                    gm = Z[128 * i:128 * i + 128, 128 * j:128 * j + 128] - acs[i] * acr[j] + vs[i] * vr[j]
                elif i < 2:
                    gm = -Pm[128 * i:128 * i + 128, :] - acs[i] * abr
                elif j < 2:
                    gm = -PT[:, 128 * j:128 * j + 128] - ab * acr[j]
                else:
                    gm = D - ab * abr
                t = 0.5 * gm * e_s[b, i, j]
                if i == j:
                    t = jnp.where(eye, 0.0, t)
                row.append(t)
            rows.append(jnp.concatenate(row, 1))
        eh, el = split(jnp.concatenate(rows, 0))
        F = f_s[pl.ds(384 * b, 384), :]
        Fo = jnp.concatenate([F, jnp.ones((384, 128), bf16)], 1)
        ef = mm(jnp.concatenate([eh, el], 1), jnp.concatenate([Fo, Fo], 0))
        cot_s[pl.ds(384 * b, 384), :] = ((-8.0 * weight / FEAT) * (ef[:, 128:] * F.astype(f32) - ef[:, :128])).astype(bf16)
    cot = cot_s[...]
    steps = sorted(
        ((dy, dx, dc) for dy in range(4) for dx in range(4) for dc in range(2) if (dy, dx, dc) != (0, 0, 0)),
        key=lambda t: -(min(t[0], 4 - t[0]) + min(t[1], 4 - t[1])),
    )
    shifted = lambda dy, dx, dc: ((here[0] + dy) % 4) * 8 + ((here[1] + dx) % 4) * 2 + (core + dc) % 2
    to = [shifted(*t) for t in steps]
    back = [shifted(4 - t[0], 4 - t[1], t[2]) for t in steps]
    updown = [4, 3, 5, 2, 6, 1, 7]
    tile = lambda m, i: m[8 * (i // 2):8 * (i // 2) + 8, 256 * (i % 2):256 * (i % 2) + 256]

    def scatter(k, pk, rs):
        for o, dev in enumerate(to):
            push(pk.at[dev], rs.at[me], rs_send.at[k, o], rs_recv.at[k, o], {"blk": dev})
        rs[me] = pk[me]

    def exchange(k, rs, part, zs):
        for o, src in enumerate(back):
            arrive(rs.at[src], rs_send.at[k, o], rs_recv.at[k, o], {"blk": partner})
        acc = rs[0].astype(f32)
        for i in range(1, 32):
            acc = acc + rs[i].astype(f32)
        part[...] = acc.astype(bf16)
        zs[z] = acc.astype(bf16)
        for o, d in enumerate(updown):
            push(part, zs.at[z], z_send.at[k, o], z_recv.at[k, o], {"grp": (z + d) % 8})

    def spread_sum(k, part, zs):
        for o, d in enumerate(updown):
            arrive(zs.at[(z + 8 - d) % 8], z_send.at[k, o], z_recv.at[k, o], {"blk": partner})
        acc = zs[0].astype(f32)
        for i in range(1, 8):
            acc = acc + zs[i].astype(f32)
        tot_out[k, me] = acc[:, :256].astype(bf16)
        for o, dev in enumerate(to):
            push(tot_out.at[k, me], tot_out.at[k, me], ag_send.at[k, o], ag_recv.at[k, o], {"blk": dev})
        return acc

    gout = t_mm(cot, hid_s[...]).astype(bf16)
    for i in range(32):
        pk_a[i] = tile(gout, i)
    scatter(0, pk_a, rs_a)
    backed = mm_t(cot, wout16) * slope_s[...]
    gin = t_mm(x_s[...], backed.astype(bf16)).astype(bf16)
    gb = jnp.sum(backed, axis=0, keepdims=True).astype(bf16)
    gb8 = jnp.concatenate([gb[:, 128 * i:128 * i + 128] for i in range(4)] + [jnp.zeros((4, 128), bf16)], 0)
    for i in range(32):
        pk_b[i] = jnp.concatenate([tile(gin, i), gb8], 1)
    scatter(1, pk_b, rs_b)

    def sweep_groups(start, count):
        def step(i, carry):
            res = eliminate_group([sw_s[b] for b in range(NB)], [sr_s[b] for b in range(NB)])
            for b in range(NB):
                sw_s[b] = res[b][0]
                sr_s[b] = res[b][1]
                ww_s[b, start + i] = res[b][2]
            return carry
        lax.fori_loop(0, count, step, 0)

    sweep_groups(0, 3)
    exchange(0, rs_a, part_a, z_a)
    exchange(1, rs_b, part_b, z_b)
    sweep_groups(3, 2)
    spread_sum(0, part_a, z_a)
    bias_out[pl.ds(0, 4), :] = spread_sum(1, part_b, z_b)[:4, 256:]
    for i in range(4):
        bias_out[pl.ds(4 + i, 1), :] = bias[:, 128 * i:128 * i + 128]
    sweep_groups(5, 3)
    for b in range(NB):
        w_out[pl.ds(b, 1), :] = torow(jnp.concatenate([ww_s[b, g] for g in range(8)], 0))
    for k in range(2):
        for o, src in enumerate(back):
            arrive(tot_out.at[k, src], ag_send.at[k, o], ag_recv.at[k, o], {"blk": partner})
    for cp in sends:
        cp.wait_send()


def main_call(nb, om, x, t, win, bin_, wout, weight):
    D = pltpu.SemaphoreType.DMA
    any_ = pl.BlockSpec(memory_space=pltpu.HBM)
    vmem = pl.BlockSpec(memory_space=V)
    return pl.pallas_call(
        functools.partial(main_kernel, weight),
        out_shape=(
            jax.ShapeDtypeStruct((2, 128), f32),
            jax.ShapeDtypeStruct((2, 32, 8, 256), bf16),
            jax.ShapeDtypeStruct((8, 128), f32),
        ),
        in_specs=[any_] * 7,
        out_specs=(vmem,) * 3,
        scratch_shapes=[
            pltpu.SMEM(nb.shape, jnp.int32), pltpu.SMEM(om.shape, jnp.int32), V(t.shape, bf16),
            V(win.shape, f32), V(bin_.shape, f32), V(wout.shape, f32),
            V((16, 2, ROWS, 128), bf16), V((4, ROWS, 128), bf16), V((4, ROWS, 128), bf16),
            V((768, 128), bf16), V((768, 512), bf16), V((768, 512), f32), V((768, 128), bf16),
            V((2, 3, 3, 128, 128), f32), V((2, 3, 3, 128, 128), f32), V((6, 128, 128), f32), V((768, 128), bf16),
            V((2, 128, 128), f32), V((2, 128, 128), f32), V((2, 8, 16, 128), f32),
            V((32, 8, 256), bf16), V((32, 8, 384), bf16), V((32, 8, 256), bf16), V((32, 8, 384), bf16),
            V((8, 256), bf16), V((8, 384), bf16), V((8, 8, 256), bf16), V((8, 8, 384), bf16),
            D((8,)), pltpu.SemaphoreType.REGULAR((3,)),
            D((2, 15)), D((2, 15)), D((2,)), D((2, 31)), D((2, 31)), D((2, 7)), D((2, 7)), D((2, 31)), D((2, 31)),
        ],
        compiler_params=pltpu.CompilerParams(collective_id=0, has_side_effects=True, vmem_limit_bytes=MAIN_VMEM),
        name="gradient_step",
    )(*(pltpu.with_memory_space_constraint(v, pltpu.HBM) for v in (nb, om, x, t, win, bin_, wout)))


def update_kernel(tot_ref, sum_ref, w_ref, win_ref, wout_ref, w_out, in_out, bias_out, out_out):
    bias = sum_ref[0:4, :]
    total = jnp.zeros((8, 256), f32)
    for k in range(2):
        for i in range(32):
            t = tot_ref[k, i].astype(f32)
            total = total + t * t
    squares = jnp.sum(total) + jnp.sum(bias * bias)
    scale = 3.0 / jnp.sqrt(jnp.broadcast_to(squares, (1, 1)) + 1e-06)
    w_out[...] = w_ref[...]
    bias_out[...] = sum_ref[4:8, :] - scale * bias
    for i in range(32):
        rows, lanes = pl.ds(8 * (i // 2), 8), pl.ds(256 * (i % 2), 256)
        in_out[rows, lanes] = win_ref[rows, lanes] - scale * tot_ref[1, i].astype(f32)
    for q in range(4):
        half, at = q // 2, 128 * (q % 2)
        t = jnp.concatenate([tot_ref[0, 2 * i + half][:, at:at + 128].astype(f32) for i in range(16)], 0)
        out_out[pl.ds(128 * q, 128), :] = wout_ref[pl.ds(128 * q, 128), :] - scale * jnp.transpose(t)


def update_call(tot, total_bias, white, win, wout):
    vmem = pl.BlockSpec(memory_space=V)
    return pl.pallas_call(
        update_kernel,
        out_shape=(
            jax.ShapeDtypeStruct((2, 128), f32),
            jax.ShapeDtypeStruct((128, 512), f32),
            jax.ShapeDtypeStruct((4, 128), f32),
            jax.ShapeDtypeStruct((512, 128), f32),
        ),
        in_specs=[vmem] * 5,
        out_specs=(vmem,) * 4,
        compiler_params=pltpu.CompilerParams(vmem_limit_bytes=8 * 1024 * 1024),
        name="update_weights",
    )(tot, total_bias, white, win, wout)


def shards(inputs, targets, weight_in, bias_in, weight_out, neighbors, owner_map):
    white, tot, total_bias = main_call(
        neighbors.T, owner_map, inputs, targets.reshape(2, PTS), weight_in, bias_in.reshape(1, -1), weight_out,
        1.0 / neighbors.shape[0],
    )
    white, new_in, new_bias, new_out = update_call(
        tot, total_bias, white, weight_in, weight_out
    )
    return (white.reshape(-1), new_in, new_bias.reshape(-1), new_out)


def solution(mesh):
    placed = (P(("grp", "blk"), None), P(("grp", "blk")), P(), P(), P(), P(), P())
    return jax.shard_map(
        shards,
        mesh=mesh,
        in_specs=placed,
        out_specs=(P(("grp", "blk")), P(), P(), P()),
        check_vma=False,
    )
```
